32 devices in a mesh: bin: 8 (over y, x, core), shard: 4 (over z).
Axes of the slice: x: 2, y: 2, z: 4, core: 2. Of those that a mesh axis runs over, the one named last changes fastest.
Arguments:
- block_input: bfloat16 [16384, 1152], P(('bin', 'shard')), may hold values from -6 to 6
- label_embed: float32 [64, 1152], P('bin'), may hold values from -6 to 6
- time_index: int32 [64], P('bin'), may hold values from 0 to 999
- segment_ids: int32 [16384], P('bin'), may hold values from 0 to 7, as said below
- ada_weight: bfloat16 [1152, 6912], replicated, may hold values from -0.1875 to 0.1875
- ada_bias: float32 [6912], replicated, may hold values from -2 to 2
- qkv_weight: bfloat16 [1152, 3456], P('bin', 'shard'), may hold values from -0.1875 to 0.1875
- qv_bias: float32 [2304], replicated, may hold values from -2 to 2
- proj_weight: bfloat16 [1152, 1152], P('bin', 'shard'), may hold values from -0.75 to 0.75
- proj_bias: float32 [1152], replicated, may hold values from -2 to 2
- up_weight: bfloat16 [1152, 4608], P('bin', 'shard'), may hold values from -0.1875 to 0.1875
- up_bias: float32 [4608], replicated, may hold values from -2 to 2
- down_weight: bfloat16 [4608, 1152], P('bin', 'shard'), may hold values from -0.09375 to 0.09375
- down_bias: float32 [1152], replicated, may hold values from -2 to 2
- bin_weight: float32 [8], P('bin'), may hold values from 0.3 to 3
- out_cotangent: bfloat16 [16384, 1152], P(('bin', 'shard')), may hold values from -6 to 6
Outputs:
- block_output: float32 [16384, 1152], P(('bin', 'shard'))
- grad_input: float32 [16384, 1152], P(('bin', 'shard'))
- grad_label: float32 [64, 1152], P('bin')
- grad_ada_weight: float32 [1152, 6912], P(None, ('bin', 'shard'))
- grad_ada_bias: float32 [6912], P(('bin', 'shard'))
- grad_qkv_weight: float32 [1152, 3456], P('bin', 'shard')
- grad_qv_bias: float32 [2304], replicated
- grad_proj_weight: float32 [1152, 1152], P('bin', 'shard')
- grad_proj_bias: float32 [1152], replicated
- grad_up_weight: float32 [1152, 4608], P('bin', 'shard')
- grad_up_bias: float32 [4608], replicated
- grad_down_weight: float32 [4608, 1152], P('bin', 'shard')
- grad_down_bias: float32 [1152], replicated
The draws below stay inside these ranges and needn't reach their ends.
Inputs may be any that keep to these rules, and one draw needn't show every extreme that they name: `segment_ids`: within each bin's group of 2048 tokens the ids number its images from 0 in order of their tokens; every image is 256 or 1024 consecutive tokens, and both sizes occur in every draw. Slots at or above a group's image count are unused.
All inputs are finite; a program needn't handle non-finite values.
Results may differ from the reference program's by a relative error of at most 0.017.
Values may be sent and summed in bfloat16 or wider, within the bound.
No kernel may reach another device: no remote copies, remote signals or barrier semaphores. Data moves between devices by JAX's collectives and lax.ppermute only.
A program may use at most 384 MiB of HBM per device.

```python
import math
import jax
import jax.numpy as jnp
from jax import lax

D = 1152
HEADS = 16
HEAD_DIM = 72
FF = 4608
IMG_SHORT = 256
BINS = 8
GROUP_TOK = 2048
IMG_GRP = 8
TOKENS = 16384
IMAGES = 64


def draw_segment_ids(key, part):
    units = GROUP_TOK // IMG_SHORT
    quads = units // 4
    key_long, key_lead = jax.random.split(jax.random.fold_in(key, 7))
    long_flags = jax.random.randint(key_long, (BINS, quads), 0, 2)
    leading = jax.random.randint(key_lead, (BINS,), 0, 4)
    group_pos = jnp.arange(BINS)
    long_flags = jnp.where(group_pos[:, None] == 0, 0, long_flags)
    long_flags = jnp.where(group_pos[:, None] == 1, 1, long_flags)
    unit_pos = jnp.arange(units)
    inner = unit_pos[None, :] - leading[:, None]
    quad_index = jnp.clip(inner // 4, 0, quads - 1)
    in_middle = (inner >= 0) & (inner < 4 * (quads - 1))
    flagged = jnp.take_along_axis(long_flags, quad_index, axis=1)
    is_long = in_middle & (flagged == 1)
    starts = jnp.where(is_long & (inner % 4 != 0), 0, 1)
    unit_segments = jnp.cumsum(starts, axis=1) - 1
    return jnp.repeat(unit_segments, IMG_SHORT, axis=1).reshape(-1).astype(jnp.int32)


def with_ends(result, rng, least, high):
    spot = [jax.random.randint(jax.random.fold_in(rng, axis), (), 0, length) for axis, length in enumerate(result.shape)]
    main_axis = result.shape.index(max(result.shape))
    neighbour = spot[:main_axis] + [(spot[main_axis] + 1) % result.shape[main_axis]] + spot[main_axis + 1:]
    return result.at[tuple(spot)].set(least).at[tuple(neighbour)].set(high)


def shard_levels(stream_key, dims, cuts, low, largest):
    factor_of = 1.0
    for axis_at, parts in cuts:
        heights = jax.random.uniform(jax.random.fold_in(jax.random.fold_in(stream_key, 6), axis_at), (parts,), jnp.float32, low / len(cuts), largest / len(cuts))
        factor_of = factor_of * jnp.repeat(jnp.exp(heights), dims[axis_at] // parts).reshape((-1,) + (1,) * (len(dims) - 1 - axis_at))
    return factor_of


def normal_values(key, shape, scale, limit, pieces=(), kind=jnp.bfloat16):
    drawn = jax.random.normal(key, shape, jnp.float32) * scale
    if len(pieces) > 0:
        drawn = shard_levels(key, shape, pieces, -0.22, 0.18) * drawn
    return jnp.clip(drawn, min=-limit, max=limit).astype(kind)


def setup_inputs(seed: int = 0) -> dict:
    seeds = jax.random.split(jax.random.key(seed), 17)
    return {
        "block_input": normal_values(seeds[0], (TOKENS, D), 1.0, 6.0, ((0, 32),)),
        "label_embed": normal_values(seeds[1], (IMAGES, D), 1.0, 6.0, ((0, 8),), jnp.float32),
        "time_index": with_ends(jax.random.randint(seeds[2], (IMAGES,), 0, 1000), jax.random.fold_in(seeds[2], 1), 0, 999).astype(jnp.int32),
        "segment_ids": draw_segment_ids(jax.random.fold_in(seeds[16], 71), 0),
        "ada_weight": normal_values(seeds[4], (D, 6 * D), D ** -0.5, 0.1875),
        "ada_bias": normal_values(seeds[5], (6 * D,), 0.3, 2.0, (), jnp.float32),
        "qkv_weight": normal_values(seeds[6], (D, 3 * D), D ** -0.5, 0.1875, ((0, 8), (1, 4))),
        "qv_bias": normal_values(seeds[7], (2 * D,), 0.3, 2.0, (), jnp.float32),
        "proj_weight": normal_values(seeds[8], (D, D), (D // 16) ** -0.5, 0.75, ((0, 8), (1, 4))),
        "proj_bias": normal_values(seeds[9], (D,), 0.3, 2.0, (), jnp.float32),
        "up_weight": normal_values(seeds[10], (D, FF), D ** -0.5, 0.1875, ((0, 8), (1, 4))),
        "up_bias": normal_values(seeds[11], (FF,), 0.3, 2.0, (), jnp.float32),
        "down_weight": normal_values(seeds[12], (FF, D), FF ** -0.5, 0.09375, ((0, 8), (1, 4))),
        "down_bias": normal_values(seeds[13], (D,), 0.3, 2.0, (), jnp.float32),
        "bin_weight": jnp.clip(jnp.exp(math.log(3.0) - 2.3025851 * jax.random.uniform(seeds[14], (BINS,), jnp.float32) ** shard_levels(seeds[14], (BINS,), ((0, 8),), -0.2, 0.2)), 0.3, 3.0),
        "out_cotangent": normal_values(seeds[15], (TOKENS, D), 1.0, 6.0, ((0, 32),)),
    }


@jax.custom_vjp
def low(v):
    return lax.optimization_barrier(v.astype(jnp.bfloat16)).astype(jnp.float32)

@jax.custom_vjp
def low_back(v):
    return v

def low_keep(v):
    return (low(v), None)

def low_pass(kept, grad):
    return (grad,)

def back_keep(v):
    return (v, None)

def back_low(kept, grad):
    return (low(grad),)
low.defvjp(low_keep, low_pass)
low_back.defvjp(back_keep, back_low)

def product(left, right):
    return jnp.dot(left, right, precision=lax.Precision.HIGHEST, preferred_element_type=jnp.float32)

def time_embed(time_index, width):
    half_width = width // 2
    freqs = jnp.exp(-math.log(10000.0) * jnp.arange(half_width, dtype=jnp.float32) / half_width)
    angles = time_index.astype(jnp.float32)[:, None] * freqs[None, :]
    return jnp.concatenate([jnp.cos(angles), jnp.sin(angles)], axis=1)

def layer_norm(value):
    center = value - lax.optimization_barrier(jnp.mean(value, axis=1, keepdims=True))
    return center * lax.rsqrt(lax.optimization_barrier(jnp.mean(center * center, axis=1, keepdims=True)) + 1e-06)

def group_forward(params, tokens, label, times, segments):
    ada_weight, ada_bias, qkv_weight, qv_bias, proj_weight, proj_bias, up_weight, up_bias, down_weight, down_bias = params
    cond = label + time_embed(times, D)
    modul = low_back(product(low(jax.nn.silu(cond)), ada_weight) + ada_bias)
    onehot = (segments[:, None] == jnp.arange(IMG_GRP, dtype=jnp.int32)[None, :]).astype(jnp.float32)
    per_token = product(onehot, modul)
    shift_a, scale_a, gate_a, shift_m, scale_m, gate_m = jnp.split(per_token, 6, axis=1)
    attn_in = low(layer_norm(tokens) * (1.0 + scale_a) + shift_a)
    qkv_bias = jnp.concatenate([qv_bias[:D], jnp.zeros((D,), jnp.float32), qv_bias[D:]])
    qkv = low(low_back(product(attn_in, qkv_weight) + qkv_bias))
    same = segments[:, None] == segments[None, :]
    score_scale = 1.0 / math.sqrt(HEAD_DIM)

    def split_heads(matrix):
        return matrix.reshape(GROUP_TOK, HEADS, HEAD_DIM).transpose(1, 0, 2)

    def one_head(operands):
        query, keys, values = operands
        scores = product(query, keys.T) * score_scale
        scores = low_back(jnp.where(same, scores, -1e+30))
        probs = jax.nn.softmax(scores, axis=1)
        return product(low(probs), values)
    heads = lax.map(jax.checkpoint(one_head), (split_heads(qkv[:, :D]), split_heads(qkv[:, D:2 * D]), split_heads(qkv[:, 2 * D:])))
    heads = low(low_back(heads.transpose(1, 0, 2).reshape(GROUP_TOK, D)))
    attn_out = low_back(product(heads, proj_weight) + proj_bias)
    middle = tokens + gate_a * attn_out
    mlp_in = low(layer_norm(middle) * (1.0 + scale_m) + shift_m)
    pre_act = low_back(product(mlp_in, up_weight) + up_bias)
    act_low = low(jax.nn.gelu(pre_act, approximate=True))
    mlp_out = low_back(product(act_low, down_weight) + down_bias)
    return middle + gate_m * mlp_out

def reference(block_input, label_embed, time_index, segment_ids, ada_weight, ada_bias, qkv_weight, qv_bias, proj_weight, proj_bias, up_weight, up_bias, down_weight, down_bias, bin_weight, out_cotangent):
    params = tuple((value.astype(jnp.float32) for value in (ada_weight, ada_bias, qkv_weight, qv_bias, proj_weight, proj_bias, up_weight, up_bias, down_weight, down_bias)))
    tokens = block_input.astype(jnp.float32).reshape(BINS, GROUP_TOK, D)
    labels = label_embed.reshape(BINS, IMG_GRP, D)
    times = time_index.reshape(BINS, IMG_GRP)
    segments = segment_ids.reshape(BINS, GROUP_TOK)

    def forward(params, tokens, labels):

        def one_group(operands):
            return group_forward(params, *operands)
        return lax.map(jax.checkpoint(one_group), (tokens, labels, times, segments))
    output, back_fn = jax.vjp(forward, params, tokens, labels)
    weighted = out_cotangent.astype(jnp.float32).reshape(BINS, GROUP_TOK, D) * bin_weight[:, None, None]
    grad_params, grad_tokens, grad_labels = back_fn(weighted)
    return (output.reshape(TOKENS, D), grad_tokens.reshape(TOKENS, D), grad_labels.reshape(IMAGES, D), grad_params[0], grad_params[1], grad_params[2], grad_params[3], grad_params[4], grad_params[5], grad_params[6], grad_params[7], grad_params[8], grad_params[9])
```

```python
import functools
import math

import jax
import jax.numpy as jnp
from jax import lax
from jax.experimental import pallas as pl
from jax.experimental.pallas import tpu as pltpu
from jax.sharding import PartitionSpec as P

HEADS = 16
HEAD_DIM = 72
BLOCK = 256
LONG = 4
BF = jnp.bfloat16
F32 = jnp.float32


def time_embed(time_index, width):
    half_width = width // 2
    freqs = jnp.exp(-math.log(10000.0) * jnp.arange(half_width, dtype=jnp.float32) / half_width)
    angles = time_index.astype(jnp.float32)[:, None] * freqs[None, :]
    return jnp.concatenate([jnp.cos(angles), jnp.sin(angles)], axis=1)


def layer_norm(value):
    center = value - jnp.mean(value, axis=-1, keepdims=True)
    inverse = lax.rsqrt(jnp.mean(center * center, axis=-1, keepdims=True) + 1e-06)
    return (center * inverse, inverse)


def norm_back(normed, inverse, grad_normed):
    mean_grad = jnp.mean(grad_normed, axis=-1, keepdims=True)
    mean_cross = jnp.mean(grad_normed * normed, axis=-1, keepdims=True)
    return inverse * (grad_normed - mean_grad - normed * mean_cross)


def dot(left, right, dims):
    return lax.dot_general(left, right, (dims, ((), ())), preferred_element_type=F32)


def per_block(rows, value):
    tokens, width = value.shape
    return jnp.broadcast_to(rows[:, None, :], (rows.shape[0], BLOCK, width)).reshape(tokens, width)


def ring(value, axis, shift):
    size = lax.axis_size(axis)
    return lax.ppermute(value, axis, [(i, (i + shift) % size) for i in range(size)])


def hop(value, axis, shift):
    size = lax.axis_size(axis)
    pairs = [(i, i + shift) for i in range(size) if 0 <= i + shift < size]
    return lax.ppermute(value, axis, pairs)


def swap(value, mask):
    size = lax.axis_size("bin")
    return lax.ppermute(value, "bin", [(i, i ^ mask) for i in range(size)])


def spread(slab, masks):
    blocks = {0: slab}
    for mask in masks:
        for key in list(blocks):
            blocks[key ^ mask] = swap(blocks[key], mask)
    return blocks


def assemble_body(count, place_ref, *refs):
    sources, out_ref, scratch, sem_in, sem_out = (
        refs[:count], refs[count], refs[count + 1], refs[count + 2], refs[count + 3])
    bin_at, shard_at = place_ref[0], place_ref[1]
    depth = count // 2
    copies = []
    for colour in range(2):
        for key in range(depth):
            for half in range(2):
                part = 2 * colour + half
                row = jnp.bitwise_xor(bin_at, key)
                column = jnp.bitwise_and(shard_at + (4 - part), 3)
                index = part * depth + key
                copy = pltpu.make_async_copy(
                    sources[colour * depth + key].at[half], scratch.at[part, key], sem_in.at[index])
                copy.start()
                copies.append((copy, scratch.at[part, key], out_ref.at[column, row], index))
    outs = []
    for copy, source, target, index in copies:
        copy.wait()
        out = pltpu.make_async_copy(source, target, sem_out.at[index])
        out.start()
        outs.append(out)
    for out in outs:
        out.wait()


def gather_weight(piece, place):
    bins, shards = lax.axis_size("bin"), lax.axis_size("shard")
    rows, columns = piece.shape
    if bins != 8 or shards != 4 or rows % 16:
        full = lax.all_gather(piece, "bin", axis=0)
        return lax.all_gather(full, "shard", axis=0)
    parts = [piece]
    for _ in range(3):
        parts.append(ring(parts[-1], "shard", 1))
    first = spread(jnp.stack(parts[:2]), [2, 4, 1])
    second = spread(jnp.stack(parts[2:]), [4, 2, 1])
    sources = [first[k] for k in range(bins)] + [second[k] for k in range(bins)]
    size = 2 * rows * columns * 32
    return pl.pallas_call(
        functools.partial(assemble_body, len(sources)),
        out_shape=jax.ShapeDtypeStruct((shards, bins, rows, columns), BF),
        in_specs=[pl.BlockSpec(memory_space=pltpu.SMEM)]
        + [pl.BlockSpec(memory_space=pl.ANY)] * len(sources),
        out_specs=pl.BlockSpec(memory_space=pl.ANY),
        scratch_shapes=[
            pltpu.VMEM((shards, bins, rows, columns), BF),
            pltpu.SemaphoreType.DMA((shards * bins,)),
            pltpu.SemaphoreType.DMA((shards * bins,)),
        ],
        compiler_params=pltpu.CompilerParams(vmem_limit_bytes=24 * 2**20),
        cost_estimate=pl.CostEstimate(flops=0, bytes_accessed=2 * size, transcendentals=0),
        name="assemble",
    )(place, *sources)


def product_body(groups, by_rows, flip, colour, place_ref, left_ref, right_ref, *refs):
    step = pl.program_id(0)
    part = step if colour is None else (step + 1 if colour == 0 else (step * 3 + 3) % 4)
    if colour == 1:
        part = jnp.where(step == 0, 3, 0)
    shard_at = jnp.bitwise_and(place_ref[1] + (4 - part), 3)
    tall = left_ref.shape[0] // (groups * 2 * (4 if by_rows else 1))
    wide = right_ref.shape[0] // (1 if by_rows else 4)
    rows = []
    for offset in range(groups):
        owner = jnp.bitwise_xor(place_ref[0], 2 * offset + flip)
        owner = owner * 4 + shard_at if by_rows else owner
        rows.append(left_ref[pl.ds(pl.multiple_of(owner * tall, 16), tall), :])
    left = jnp.concatenate(rows, axis=0)
    if by_rows:
        right = right_ref[...]
    else:
        right = right_ref[pl.ds(pl.multiple_of(shard_at * wide, 16), wide), :]
    result = dot(left, right, ((1,), (1,))).reshape(groups, tall, wide)
    if colour is None:
        refs[0][:, 0] = result.astype(BF)
        return
    result = result + refs[0][:, 0].astype(F32)
    bit = 1 if colour == 0 else groups // 2
    sent = [o for o in range(groups) if o & bit]
    kept = [o for o in range(groups) if not o & bit]
    for at, offset in enumerate(sent):
        refs[1][at, 0] = result[offset].astype(BF)
    for at, offset in enumerate(kept):
        refs[2][at, 0] = result[offset].astype(BF)


def product(place, left, right, by_rows, colour, arrived=None):
    groups = lax.axis_size("bin") // 2
    tall = left.shape[0] // (groups * 2 * (4 if by_rows else 1))
    wide = right.shape[0] // (1 if by_rows else 4)
    steps = 4 if colour is None else 2
    whole = lambda step, place_ref: (0, 0)
    block = lambda n: pl.BlockSpec((n, 1, tall, wide), lambda step, place_ref: (0, step, 0, 0))
    specs = [pl.BlockSpec(left.shape, whole), pl.BlockSpec(right.shape, whole)]
    operands = [left, right]
    if colour is None:
        shapes = jax.ShapeDtypeStruct((groups, 4, tall, wide), BF)
        out_specs = block(groups)
    else:
        half = jax.ShapeDtypeStruct((groups // 2, 2, tall, wide), BF)
        shapes = (half, half)
        out_specs = (block(groups // 2), block(groups // 2))
        index = (lambda step, place_ref: (0, step + 1, 0, 0)) if colour == 0 else (
            lambda step, place_ref: (0, 3 - 3 * step, 0, 0))
        specs.append(pl.BlockSpec((groups, 1, tall, wide), index))
        operands.append(arrived)
    flops = 2 * groups * steps * tall * wide * left.shape[1]
    moved = 2 * (left.size + right.size + groups * steps * tall * wide * (1 if colour is None else 2))
    return pl.pallas_call(
        functools.partial(product_body, groups, by_rows, 1 if colour is None else 0, colour),
        out_shape=shapes,
        grid_spec=pltpu.PrefetchScalarGridSpec(
            num_scalar_prefetch=1, grid=(steps,), in_specs=specs, out_specs=out_specs),
        compiler_params=pltpu.CompilerParams(vmem_limit_bytes=48 * 2**20),
        cost_estimate=pl.CostEstimate(flops=flops, bytes_accessed=moved, transcendentals=0),
        name="gradient",
    )(place, *operands)


def wide_sum(*terms):
    total = terms[0].astype(F32)
    for term in terms[1:]:
        total = total + term.astype(F32)
    return total


def scatter_gradient(place, left, right, by_rows=False):
    bins, shards = lax.axis_size("bin"), lax.axis_size("shard")
    tall = left.shape[0] // bins // (4 if by_rows else 1)
    if bins != 8 or shards != 4 or tall % 16:
        full = dot(left, right, ((1,), (1,))).astype(BF)
        shorter = lax.psum_scatter(full, "bin", scatter_dimension=0, tiled=True)
        return lax.psum_scatter(shorter, "shard", scatter_dimension=1, tiled=True).astype(F32)
    arrived = swap(product(place, left, right, by_rows, None), 1)
    kept = []
    for colour, masks in ((0, (2, 4)), (1, (4, 2))):
        sent, held = product(place, left, right, by_rows, colour, arrived)
        came = swap(sent, masks[0])
        came_last = swap(wide_sum(held[1], came[1]).astype(BF), masks[1])
        kept.append((held[0], came[0], came_last))
    piece = lambda colour, at: wide_sum(*[term[at] for term in kept[colour]])
    moving = ring(piece(0, 0).astype(BF), "shard", 1)
    moving = ring((piece(0, 1) + moving).astype(BF), "shard", 1)
    moving = ring((piece(1, 0) + moving).astype(BF), "shard", 1)
    total = piece(1, 1) + moving
    if by_rows:
        return lax.all_to_all(
            total.astype(BF), "shard", split_axis=1, concat_axis=0, tiled=True).astype(F32)
    return total


def probabilities(keys, query):
    scores = dot(keys, query, ((0,), (0,))) * (1.0 / math.sqrt(HEAD_DIM))
    expo = jnp.exp(scores - jnp.max(scores, axis=0, keepdims=True))
    return expo, jnp.sum(expo, axis=0, keepdims=True)


def blocks_of(ref, slots, first):
    return jnp.concatenate(
        [ref[0, :, pl.ds(pl.multiple_of(s * BLOCK, BLOCK), BLOCK)] for s in slots], axis=1)


def each_image(plan_ref, at, work):
    single = plan_ref[at, 0] == 1

    @pl.when(single)
    def _():
        work([plan_ref[at, 1]])

    @pl.when(jnp.logical_not(single))
    def _():
        work([plan_ref[at, 1 + i] for i in range(LONG)])


def attend_body(plan_ref, query_ref, keys_ref, values_ref, out_ref):
    for at in range(query_ref.shape[2] // BLOCK):
        here = pl.ds(at * BLOCK, BLOCK)

        def work(slots):
            expo, total = probabilities(blocks_of(keys_ref, slots, 0), query_ref[0, :, here])
            probs = (expo / total).astype(BF)
            out = dot(blocks_of(values_ref, slots, 0), probs, ((1,), (0,)))
            out_ref[0, :, here] = out.astype(BF)

        each_image(plan_ref, at, work)


def attend_back_body(
    plan_ref, query_ref, keys_ref, values_ref, grad_ref, dq_ref, dk_ref, dv_ref, dk_sum, dv_sum
):
    dk_sum[...] = jnp.zeros_like(dk_sum)
    dv_sum[...] = jnp.zeros_like(dv_sum)
    scale = 1.0 / math.sqrt(HEAD_DIM)
    for at in range(query_ref.shape[2] // BLOCK):
        here = pl.ds(at * BLOCK, BLOCK)

        def work(slots):
            query = query_ref[0, :, here]
            grad = grad_ref[0, :, here]
            keys = blocks_of(keys_ref, slots, 0)
            expo, total = probabilities(keys, query)
            probs = expo / total
            grad_probs = dot(blocks_of(values_ref, slots, 0), grad, ((0,), (0,)))
            delta = jnp.sum(grad_probs * probs, axis=0, keepdims=True)
            grad_scores = (probs * (grad_probs - delta)).astype(BF)
            dq_ref[0, :, here] = (dot(keys, grad_scores, ((1,), (0,))) * scale).astype(BF)
            dk = dot(query, grad_scores, ((1,), (1,))) * scale
            dv = dot(grad, probs.astype(BF), ((1,), (1,)))
            for i, slot in enumerate(slots):
                there = pl.ds(pl.multiple_of(slot * BLOCK, BLOCK), BLOCK)
                dk_sum[:, there] += dk[:, i * BLOCK:(i + 1) * BLOCK]
                dv_sum[:, there] += dv[:, i * BLOCK:(i + 1) * BLOCK]

        each_image(plan_ref, at, work)
    dk_ref[0] = dk_sum[...].astype(BF)
    dv_ref[0] = dv_sum[...].astype(BF)


def head_spec(tokens, first=0):
    return pl.BlockSpec((1, HEAD_DIM, tokens), lambda head, plan_ref: (head + first, 0, 0))


def attend(plan, queries, keys_values):
    tokens, window = queries.shape[2], keys_values.shape[2]
    return pl.pallas_call(
        attend_body,
        out_shape=jax.ShapeDtypeStruct((HEADS, HEAD_DIM, tokens), BF),
        grid_spec=pltpu.PrefetchScalarGridSpec(
            num_scalar_prefetch=1,
            grid=(HEADS,),
            in_specs=[head_spec(tokens), head_spec(window), head_spec(window, HEADS)],
            out_specs=head_spec(tokens),
        ),
        compiler_params=pltpu.CompilerParams(vmem_limit_bytes=40 * 2**20),
        cost_estimate=pl.CostEstimate(
            flops=4 * HEADS * tokens * 1024 * 256, bytes_accessed=6 * 2**20, transcendentals=0),
        name="attend",
    )(plan, queries, keys_values, keys_values)


def attend_back(plan, queries, keys_values, grads):
    tokens, window = queries.shape[2], keys_values.shape[2]
    shape = lambda n: jax.ShapeDtypeStruct((HEADS, HEAD_DIM, n), BF)
    return pl.pallas_call(
        attend_back_body,
        out_shape=(shape(tokens), shape(window), shape(window)),
        grid_spec=pltpu.PrefetchScalarGridSpec(
            num_scalar_prefetch=1,
            grid=(HEADS,),
            in_specs=[
                head_spec(tokens), head_spec(window), head_spec(window, HEADS), head_spec(tokens)],
            out_specs=(head_spec(tokens), head_spec(window), head_spec(window)),
            scratch_shapes=[pltpu.VMEM((HEAD_DIM, window), F32), pltpu.VMEM((HEAD_DIM, window), F32)],
        ),
        compiler_params=pltpu.CompilerParams(vmem_limit_bytes=48 * 2**20),
        cost_estimate=pl.CostEstimate(
            flops=10 * HEADS * tokens * 1024 * 256, bytes_accessed=12 * 2**20, transcendentals=0),
        name="attend_back",
    )(plan, queries, keys_values, keys_values, grads)


def plan_of(block_segments, first, own_blocks, shards):
    at = lax.axis_index("shard")
    count = block_segments.shape[0]
    numbers = jnp.arange(count, dtype=jnp.int32)
    rows = []
    for i in range(own_blocks):
        mine = block_segments[first + i]
        same = block_segments == mine
        begin = jnp.argmax(same).astype(jnp.int32)
        size = jnp.sum(same.astype(jnp.int32))
        cells = [jnp.where(size == 1, 1, LONG)]
        for j in range(LONG):
            block = jnp.minimum(begin + j, count - 1)
            owner = block // own_blocks
            inside = block % own_blocks
            slot = jnp.where(
                owner == at, inside,
                jnp.where(owner == at - 1, own_blocks + inside,
                          jnp.where(owner == at + 1, 2 * own_blocks + inside, 3 * own_blocks)))
            cells.append(slot)
        rows.append(jnp.stack(cells))
    far = jnp.where(at < shards // 2, (at + 2) * own_blocks, (at - 2) * own_blocks + own_blocks - 1)
    window = [first + i for i in range(own_blocks)]
    window += [first - own_blocks + i for i in range(own_blocks)]
    window += [first + own_blocks + i for i in range(own_blocks)]
    window = jnp.clip(jnp.stack(window + [far]), 0, count - 1)
    return jnp.stack(rows).astype(jnp.int32), window


def per_device(
    block_input,
    label_embed,
    time_index,
    segment_ids,
    ada_weight,
    ada_bias,
    qkv_weight,
    qv_bias,
    proj_weight,
    proj_bias,
    up_weight,
    up_bias,
    down_weight,
    down_bias,
    bin_weight,
    out_cotangent,
):
    tokens, width = block_input.shape
    slots = label_embed.shape[0]
    bins, shards = lax.axis_size("bin"), lax.axis_size("shard")
    bin_at, shard_at = lax.axis_index("bin"), lax.axis_index("shard")
    place = jnp.stack([bin_at, shard_at]).astype(jnp.int32)
    own_blocks = tokens // BLOCK
    lower = shard_at < shards // 2

    from_left = hop(block_input, "shard", 1)
    from_right = hop(block_input, "shard", -1)
    edge = jnp.where(lower, block_input[tokens - BLOCK:], block_input[:BLOCK])
    across = ring(edge, "shard", 2)

    qkv_parts = gather_weight(qkv_weight, place)
    proj_parts = gather_weight(proj_weight, place)
    up_parts = gather_weight(up_weight, place)
    down_rows = lax.all_to_all(down_weight, "shard", split_axis=0, concat_axis=1, tiled=True)
    down_parts = gather_weight(down_rows, place)
    full = lambda parts: parts.transpose(1, 2, 0, 3).reshape(
        bins * parts.shape[2], shards * parts.shape[3])
    qkv_full, proj_full, up_full = full(qkv_parts), full(proj_parts), full(up_parts)
    down_full = down_parts.transpose(1, 0, 2, 3).reshape(4 * width, width)

    cond = label_embed + time_embed(time_index, width)
    cond_low = jax.nn.silu(cond).astype(BF)
    modul = dot(cond_low, ada_weight, ((1,), (0,))) + ada_bias
    block_segments = segment_ids[::BLOCK]
    first = shard_at * own_blocks
    plan, window_blocks = plan_of(block_segments, first, own_blocks, shards)
    picked = (block_segments[window_blocks][:, None] == jnp.arange(slots, dtype=jnp.int32)[None, :]).astype(F32)
    rows = jnp.dot(picked, modul, precision=lax.Precision.HIGHEST, preferred_element_type=F32)
    own_rows = jnp.split(rows[:own_blocks], 6, axis=1)
    shift_a, scale_a, gate_a, shift_m, scale_m, gate_m = [
        row.reshape(own_blocks, 1, width) for row in own_rows]
    window_shift = rows[:, None, :width]
    window_scale = rows[:, None, width:2 * width]

    stacked = jnp.concatenate([block_input, from_left, from_right, across], axis=0)
    span = stacked.shape[0] // BLOCK
    in_blocks = lambda value: value.reshape(value.shape[0] // BLOCK, BLOCK, value.shape[1])
    flat = lambda value: value.reshape(value.shape[0] * BLOCK, value.shape[2])
    window_normed = layer_norm(in_blocks(stacked).astype(F32))[0]
    window_in = flat((window_normed * (1.0 + window_scale) + window_shift).astype(BF))
    x = in_blocks(block_input).astype(F32)
    normed, inverse = layer_norm(x)
    attn_in = window_in[:tokens]
    query = (dot(qkv_full[:, :width], attn_in, ((0,), (1,))) + qv_bias[:width, None]).astype(BF)
    kv_bias = jnp.concatenate([jnp.zeros((width,), F32), qv_bias[width:]])
    key_value = (dot(qkv_full[:, width:], window_in, ((0,), (1,))) + kv_bias[:, None]).astype(BF)
    query = query.reshape(HEADS, HEAD_DIM, tokens)
    key_value = key_value.reshape(2 * HEADS, HEAD_DIM, span * BLOCK)
    heads = attend(plan, query, key_value).reshape(width, tokens)
    attn_out = in_blocks(dot(heads, proj_full, ((0,), (0,))) + proj_bias)
    middle = x + gate_a * attn_out
    normed_mlp, inverse_mlp = layer_norm(middle)
    mlp_in = flat((normed_mlp * (1.0 + scale_m) + shift_m).astype(BF))
    pre_act = dot(mlp_in, up_full, ((1,), (0,))) + up_bias
    act_low = jax.nn.gelu(pre_act, approximate=True).astype(BF)
    mlp_out = in_blocks(dot(act_low, down_full, ((1,), (0,))) + down_bias)
    result = middle + gate_m * mlp_out

    grad_out = in_blocks(out_cotangent).astype(F32) * bin_weight[0]
    grad_mlp = flat((grad_out * gate_m).astype(BF))
    grad_down = scatter_gradient(place, act_low.T, grad_mlp.T, by_rows=True)
    grad_down_b = jnp.sum(grad_mlp.astype(F32), axis=0)
    grad_act = dot(grad_mlp, down_full, ((1,), (1,)))
    gelu_back = jax.vjp(lambda value: jax.nn.gelu(value, approximate=True), pre_act)[1]
    grad_pre = gelu_back(grad_act)[0].astype(BF)
    grad_up = scatter_gradient(place, mlp_in.T, grad_pre.T)
    grad_up_b = jnp.sum(grad_pre.astype(F32), axis=0)
    grad_in_mlp = in_blocks(dot(grad_pre, up_full, ((1,), (1,))))
    grad_mid = grad_out + norm_back(normed_mlp, inverse_mlp, grad_in_mlp * (1.0 + scale_m))
    grad_attn = flat((grad_mid * gate_a).astype(BF))
    grad_proj = scatter_gradient(place, heads, grad_attn.T)
    grad_proj_b = jnp.sum(grad_attn.astype(F32), axis=0)
    grad_heads = dot(proj_full, grad_attn, ((1,), (1,))).astype(BF).reshape(HEADS, HEAD_DIM, tokens)
    dq, dk, dv = attend_back(plan, query, key_value, grad_heads)
    rest = span * BLOCK - tokens
    dq = dq.reshape(width, tokens)
    grad_kv = jnp.concatenate([dk.reshape(width, -1), dv.reshape(width, -1)], axis=0)
    grad_qkv = jnp.concatenate(
        [jnp.pad(dq, ((0, 0), (0, rest))), grad_kv], axis=0)
    away = dot(grad_kv[:, tokens:], qkv_full[:, width:], ((0,), (1,))).astype(BF)
    home = dot(grad_qkv[:, :tokens], qkv_full, ((0,), (1,)))
    back_left = hop(away[:tokens], "shard", -1)
    back_right = hop(away[tokens:2 * tokens], "shard", 1)
    back_edge = ring(away[2 * tokens:], "shard", 2).astype(F32)
    none = jnp.zeros((tokens - BLOCK, width), F32)
    back_edge = jnp.where(
        lower, jnp.concatenate([none, back_edge]), jnp.concatenate([back_edge, none]))
    grad_in_attn = in_blocks(home + back_left.astype(F32) + back_right.astype(F32) + back_edge)
    grad_qkv_w = scatter_gradient(place, window_in.T, grad_qkv)
    grad_qv_b = jnp.concatenate(
        [jnp.sum(dq.astype(F32), axis=1), jnp.sum(grad_kv[width:].astype(F32), axis=1)])
    grad_input = grad_mid + norm_back(normed, inverse, grad_in_attn * (1.0 + scale_a))

    sums = jnp.concatenate(
        [
            jnp.sum(term, axis=1)
            for term in (
                grad_in_attn,
                grad_in_attn * normed,
                grad_mid * attn_out,
                grad_in_mlp,
                grad_in_mlp * normed_mlp,
                grad_out * mlp_out,
            )
        ],
        axis=1,
    )
    grad_mod_part = lax.dot_general(
        picked[:own_blocks], sums, (((0,), (0,)), ((), ())),
        precision=lax.Precision.HIGHEST, preferred_element_type=F32)
    grad_mod = lax.psum(grad_mod_part, "shard").astype(BF)
    grad_cond_act = dot(grad_mod, ada_weight, ((1,), (1,)))
    grad_label = jax.vjp(jax.nn.silu, cond)[1](grad_cond_act)[0]
    own_width = grad_mod.shape[1] // (bins * shards)
    mod_view = grad_mod.reshape(slots, bins, shards, own_width)
    columns = lax.dynamic_index_in_dim(mod_view, shard_at, axis=2, keepdims=False)
    columns = lax.all_gather(columns, "bin", axis=0)
    columns = lax.dynamic_index_in_dim(columns, bin_at, axis=2, keepdims=False)
    columns = columns.reshape(bins * slots, own_width)
    cond_all = lax.all_gather(cond_low, "bin", axis=0, tiled=True)
    grad_ada_w = dot(cond_all, columns, ((0,), (0,)))
    grad_ada_b = jnp.sum(columns.astype(F32), axis=0)
    bias_sums = lax.psum((grad_qv_b, grad_proj_b, grad_up_b, grad_down_b), ("bin", "shard"))
    return (
        flat(result),
        flat(grad_input),
        grad_label,
        grad_ada_w,
        grad_ada_b,
        grad_qkv_w,
        bias_sums[0],
        grad_proj,
        bias_sums[1],
        grad_up,
        bias_sums[2],
        grad_down,
        bias_sums[3],
    )


def solution(mesh):
    placed = (
        P(("bin", "shard"), None),
        P("bin", None),
        P("bin"),
        P("bin"),
        P(),
        P(),
        P("bin", "shard"),
        P(),
        P("bin", "shard"),
        P(),
        P("bin", "shard"),
        P(),
        P("bin", "shard"),
        P(),
        P("bin"),
        P(("bin", "shard"), None),
    )
    return jax.shard_map(
        per_device,
        mesh=mesh,
        in_specs=placed,
        out_specs=(
            P(("bin", "shard"), None),
            P(("bin", "shard"), None),
            P("bin", None),
            P(None, ("bin", "shard")),
            P(("bin", "shard")),
            P("bin", "shard"),
            P(),
            P("bin", "shard"),
            P(),
            P("bin", "shard"),
            P(),
            P("bin", "shard"),
            P(),
        ),
        check_vma=False,
    )
```
